32 devices in a mesh: rep: 8 (over z, y), shard: 4 (over x, core).
Axes of the slice: x: 2, y: 2, z: 4, core: 2. Of those that a mesh axis runs over, the one named last changes fastest.
Arguments:
- layer_input: bfloat16 [32, 1024, 1152], P(('rep', 'shard')), may hold values from -6 to 6
- segments: int32 [32, 1024], P(('rep', 'shard')), may hold values from 0 to 15, never falling along the last dimension, each value on 1 to 512 neighbouring positions
- query_weight: bfloat16 [1152, 1152], P('shard'), may hold values from -0.25 to 0.25
- key_weight: bfloat16 [1152, 384], P('shard'), may hold values from -0.25 to 0.25
- value_weight: bfloat16 [1152, 384], P('shard'), may hold values from -0.1875 to 0.1875
- output_weight: bfloat16 [1152, 1152], P('shard'), may hold values from -0.75 to 0.75
- gate_weight: bfloat16 [1152, 3072], P('shard'), may hold values from -0.1875 to 0.1875
- up_weight: bfloat16 [1152, 3072], P('shard'), may hold values from -0.1875 to 0.1875
- down_weight: bfloat16 [3072, 1152], P('shard'), may hold values from -0.109375 to 0.109375
- attention_gain: bfloat16 [1152], P('shard'), may hold values from 0.5 to 1.5
- feedforward_gain: bfloat16 [1152], P('shard'), may hold values from 0.5 to 1.5
- upstream: bfloat16 [32, 1024, 1152], P(('rep', 'shard')), may hold values from -6 to 6
Outputs:
- layer_output: bfloat16 [32, 1024, 1152], P(('rep', 'shard'))
- input_grad: float32 [32, 1024, 1152], P(('rep', 'shard'))
- query_grad: float32 [1152, 1152], P('shard')
- key_grad: float32 [1152, 384], P('shard')
- value_grad: float32 [1152, 384], P('shard')
- output_grad: float32 [1152, 1152], P('shard')
- gate_grad: float32 [1152, 3072], P('shard')
- up_grad: float32 [1152, 3072], P('shard')
- down_grad: float32 [3072, 1152], P('shard')
- attention_gain_grad: float32 [1152], P('shard')
- feedforward_gain_grad: float32 [1152], P('shard')
- head_maxima: float32 [18], replicated
- query_clipped: float32 [1152, 1152], P('shard')
- key_clipped: float32 [1152, 384], P('shard')
The draws below stay inside these ranges and needn't reach their ends.
Inputs may be any that keep to these rules, and one draw needn't show every extreme that they name: `segments`: segment numbers never fall along a sequence; each document has 1 to 512 tokens.
All inputs are finite; a program needn't handle non-finite values.
Results may differ from the reference program's by a relative error of at most 0.017.
Values may be sent and summed in bfloat16 or wider, within the bound.
A program may use at most 384 MiB of HBM per device.

```python
import math
import jax
import jax.numpy as jnp
import numpy as np
from jax import lax

D = 1152
HEADS = 18
KV_HEADS = 6
HEAD_DIM = 64
FF = 3072
SEQ = 1024
DOCS = 16
MOST_DOC = 512
NSEQ = 32


def head_scaled(key, head_count, scale_low, scale_high):
    scale_key = jax.random.fold_in(key, 11)
    entry_key = jax.random.fold_in(key, 23)
    head_scale = jnp.exp(jax.random.uniform(scale_key, (head_count,), jnp.float32, math.log(scale_low), math.log(scale_high)))
    entries = jax.random.truncated_normal(entry_key, -4.0, 4.0, (D, head_count, HEAD_DIM), jnp.float32)
    scaled = entries * head_scale[None, :, None] * math.sqrt(2.0 / D)
    return scaled.reshape(D, head_count * HEAD_DIM).astype(jnp.bfloat16)


def draw_query_weight(key, part):
    return head_scaled(key, HEADS, 0.5, 1.4)


def draw_key_weight(key, part):
    return head_scaled(jax.random.fold_in(key, 5), KV_HEADS, 0.7, 1.3)


def block_levels(own_key, extent, cuts, least, high):
    level = 1.0
    for dim, shards_of in cuts:
        heights = jax.random.uniform(jax.random.fold_in(jax.random.fold_in(own_key, 6), dim), (shards_of,), jnp.float32, least / len(cuts), high / len(cuts))
        level = level * jnp.repeat(jnp.exp(heights), extent[dim] // shards_of).reshape((-1,) + (1,) * (len(extent) - 1 - dim))
    return level


def length_profile(number_of, total, reach, lean):
    weights = [(1 << 20) // math.isqrt(standing ** lean) + 1 for standing in range(2, number_of + 1)]
    surplus, holding = total - reach - (number_of - 1), [1] * (number_of - 1)
    while surplus > 0:
        free = [i for i in range(number_of - 1) if holding[i] < reach]
        mass, budget = sum([weights[i] for i in free]), surplus
        for i in free:
            extra = min(reach - holding[i], max(1, budget * weights[i] // mass), surplus)
            holding[i] = holding[i] + extra
            surplus = surplus - extra
    return np.array([reach] + holding)


def ragged(rng, count, total, limit, slope):
    if count == 2:
        one = jax.random.randint(rng, (), max(1, total - limit), min(limit, total - 1) + 1)
        return jnp.stack([one, total - one])
    tallies = jnp.asarray(length_profile(count, total, limit, slope), jnp.int32)
    pairs = (count - 1) // 2
    source_of, receiver = tallies[1:1 + 2 * pairs:2], tallies[2:2 + 2 * pairs:2]
    slack = jnp.minimum(source_of - 1, limit - receiver)
    passed = jax.random.randint(jax.random.fold_in(rng, 1), (pairs,), 0, 1 << 20) % (slack + 1)
    tallies = tallies.at[1:1 + 2 * pairs:2].set(source_of - passed).at[2:2 + 2 * pairs:2].set(receiver + passed)
    return tallies[jax.random.permutation(jax.random.fold_in(rng, 2), count)]


def gaussian(stream_key, dims, width, most, pieces=(), kind=jnp.bfloat16):
    array = width * jax.random.normal(stream_key, dims, jnp.float32)
    if pieces:
        array = array * block_levels(stream_key, dims, pieces, -0.22, 0.18)
    return jnp.clip(array, -most, most).astype(kind)


def setup_inputs(seed: int = 0) -> dict:
    seeds = jax.random.split(jax.random.key(seed), 13)
    return {
        "layer_input": gaussian(seeds[0], (NSEQ, SEQ, D), 1.0, 6.0, ((0, 32),)),
        "segments": jax.vmap(lambda own: jnp.searchsorted(jnp.cumsum(ragged(own, DOCS, SEQ, MOST_DOC, 3)), jnp.arange(SEQ), side="right"))(jax.random.split(seeds[1], NSEQ)).reshape((NSEQ, SEQ)).astype(jnp.int32),
        "query_weight": draw_query_weight(jax.random.fold_in(seeds[12], 71), 0),
        "key_weight": draw_key_weight(jax.random.fold_in(seeds[12], 71), 0),
        "value_weight": gaussian(seeds[4], (D, KV_HEADS * HEAD_DIM), D ** -0.5, 0.1875, ((0, 4),)),
        "output_weight": gaussian(seeds[5], (HEADS * HEAD_DIM, D), (HEADS * HEAD_DIM // 16) ** -0.5, 0.75, ((0, 4),)),
        "gate_weight": gaussian(seeds[6], (D, FF), D ** -0.5, 0.1875, ((0, 4),)),
        "up_weight": gaussian(seeds[7], (D, FF), D ** -0.5, 0.1875, ((0, 4),)),
        "down_weight": gaussian(seeds[8], (FF, D), FF ** -0.5, 0.109375, ((0, 4),)),
        "attention_gain": jnp.clip(1.0 + 0.1 * jax.random.normal(seeds[9], (D,), jnp.float32), 0.5, 1.5).astype(jnp.bfloat16),
        "feedforward_gain": jnp.clip(1.0 + 0.1 * jax.random.normal(seeds[10], (D,), jnp.float32), 0.5, 1.5).astype(jnp.bfloat16),
        "upstream": gaussian(seeds[11], (NSEQ, SEQ, D), 1.0, 6.0, ((0, 32),)),
    }


@jax.custom_vjp
def low(v):
    return lax.optimization_barrier(v.astype(jnp.bfloat16)).astype(jnp.float32)

@jax.custom_vjp
def low_back(v):
    return v

def low_keep(v):
    return (low(v), None)

def low_pass(kept, grad):
    return (grad,)

def back_keep(v):
    return (v, None)

def back_low(kept, grad):
    return (low(grad),)
low.defvjp(low_keep, low_pass)
low_back.defvjp(back_keep, back_low)
eps_norm = 1e-05
rope_base = 10000.0
clip_tau = 2.5
mask_fill = -1000000000.0
floor_fill = -1e+30

def matmul_high(left, right):
    return jnp.dot(left, right, precision=lax.Precision.HIGHEST, preferred_element_type=jnp.float32)

def positions_of(segment_row):
    position_index = jnp.arange(segment_row.shape[0], dtype=jnp.int32)
    changed = jnp.concatenate([jnp.ones((1,), dtype=jnp.bool_), segment_row[1:] != segment_row[:-1]])
    starts = lax.cummax(jnp.where(changed, position_index, 0).astype(jnp.int32), axis=0)
    return position_index - starts

def rope_tables(places):
    half_size = HEAD_DIM // 2
    frequency = rope_base ** (-jnp.arange(half_size, dtype=jnp.float32) * 2.0 / HEAD_DIM)
    angles = places.astype(jnp.float32)[:, None] * frequency[None, :]
    return (jnp.cos(angles)[:, None, :], jnp.sin(angles)[:, None, :])

def rotate(values_in, cosine, sine, head_count):
    row_count = values_in.shape[0]
    half_size = HEAD_DIM // 2
    shaped = values_in.reshape(row_count, head_count, HEAD_DIM)
    first_half = shaped[..., :half_size]
    second_half = shaped[..., half_size:]
    turned = jnp.concatenate([first_half * cosine - second_half * sine, second_half * cosine + first_half * sine], axis=-1)
    return turned.reshape(row_count, head_count * HEAD_DIM)

def layer_sequence(inputs, segment_row, weights):
    query_weight, key_weight, value_weight, output_weight, gate_weight, up_weight, down_weight, attention_gain, feedforward_gain = weights
    length = inputs.shape[0]
    group_size = HEADS // KV_HEADS
    score_scale = 1.0 / math.sqrt(HEAD_DIM)
    cosine, sine = rope_tables(positions_of(segment_row))
    first_rstd = lax.rsqrt(lax.optimization_barrier(jnp.mean(inputs * inputs, axis=-1, keepdims=True)) + eps_norm)
    first_normed = low(inputs * first_rstd * attention_gain)
    queries = low(rotate(low_back(matmul_high(first_normed, query_weight)), cosine, sine, HEADS))
    keys = low(rotate(low_back(matmul_high(first_normed, key_weight)), cosine, sine, KV_HEADS))
    values = low(low_back(matmul_high(first_normed, value_weight)))
    query_heads = queries.reshape(length, KV_HEADS, group_size, HEAD_DIM)
    key_heads = keys.reshape(length, KV_HEADS, HEAD_DIM)
    value_heads = values.reshape(length, KV_HEADS, HEAD_DIM)
    raw_scores = jnp.einsum('qgrd,kgd->grqk', query_heads, key_heads, precision=lax.Precision.HIGHEST)
    scores = low_back(raw_scores) * score_scale
    position_index = jnp.arange(length, dtype=jnp.int32)
    allowed = (segment_row[:, None] == segment_row[None, :]) & (position_index[None, :] <= position_index[:, None])
    head_top = lax.optimization_barrier(jnp.max(jnp.where(allowed, scores, floor_fill), axis=(2, 3))).reshape(HEADS)
    masked = jnp.where(allowed, scores, mask_fill)
    row_peaks = lax.optimization_barrier(jnp.max(masked, axis=-1, keepdims=True))
    exponents = jnp.exp(masked - row_peaks)
    softmax_weights = exponents / lax.optimization_barrier(jnp.sum(exponents, axis=-1, keepdims=True))
    mixed_heads = jnp.einsum('grqk,kgd->qgrd', low(softmax_weights), value_heads, precision=lax.Precision.HIGHEST)
    mixed = low_back(low(mixed_heads.reshape(length, HEADS * HEAD_DIM)))
    residual = inputs + low_back(matmul_high(mixed, output_weight))
    second_rstd = lax.rsqrt(lax.optimization_barrier(jnp.mean(residual * residual, axis=-1, keepdims=True)) + eps_norm)
    second_normed = low(residual * second_rstd * feedforward_gain)
    gate_values = low_back(matmul_high(second_normed, gate_weight))
    up_values = low_back(matmul_high(second_normed, up_weight))
    activated = low(gate_values * jax.nn.sigmoid(gate_values) * up_values)
    return (residual + low_back(matmul_high(activated, down_weight)), head_top)

def forward_all(inputs, segments, weights):
    rolled = jax.checkpoint(layer_sequence)

    def scan_step(carry_value, item_pair):
        out_sequence, top_sequence = rolled(item_pair[0], item_pair[1], weights)
        return (carry_value, (out_sequence, top_sequence))
    carry_zero = jnp.zeros((), jnp.float32)
    unused, (outputs, top_values) = lax.scan(scan_step, carry_zero, (inputs, segments))
    return (outputs, lax.optimization_barrier(jnp.max(top_values, axis=0)))

def reference(layer_input, segments, query_weight, key_weight, value_weight, output_weight, gate_weight, up_weight, down_weight, attention_gain, feedforward_gain, upstream):
    weights = tuple((weight.astype(jnp.float32) for weight in (query_weight, key_weight, value_weight, output_weight, gate_weight, up_weight, down_weight, attention_gain, feedforward_gain)))
    inputs = layer_input.astype(jnp.float32)

    def wrapped(inputs_now, *weight_list):
        return forward_all(inputs_now, segments, weight_list)
    outputs, pullback, maxima = jax.vjp(wrapped, inputs, *weights, has_aux=True)
    gradients = pullback(upstream.astype(jnp.float32))
    group_size = HEADS // KV_HEADS
    query_factor = jnp.sqrt(clip_tau / jnp.maximum(maxima, clip_tau))
    key_factor = jnp.sqrt(clip_tau / jnp.maximum(lax.optimization_barrier(jnp.max(maxima.reshape(KV_HEADS, group_size), axis=1)), clip_tau))
    query_clipped = (weights[0].reshape(D, HEADS, HEAD_DIM) * query_factor[None, :, None]).reshape(D, HEADS * HEAD_DIM)
    key_clipped = (weights[1].reshape(D, KV_HEADS, HEAD_DIM) * key_factor[None, :, None]).reshape(D, KV_HEADS * HEAD_DIM)
    return (outputs.astype(jnp.bfloat16), gradients[0], gradients[1], gradients[2], gradients[3], gradients[4], gradients[5], gradients[6], gradients[7], gradients[8], gradients[9], maxima, query_clipped, key_clipped)
```

```python
import functools
import math

import jax
import jax.numpy as jnp
from jax import lax
from jax.experimental import pallas as pl
from jax.experimental.pallas import tpu as pltpu
from jax.sharding import PartitionSpec as P

HEADS = 18
KV_HEADS = 6
MOST_DOC = 512
eps_norm = 1e-05
rope_base = 10000.0
clip_tau = 2.5
HEAD_DIM = 64
TQ = 128
f32 = jnp.float32
bf16 = jnp.bfloat16
NT = (((1,), (1,)), ((), ()))
NN = (((1,), (0,)), ((), ()))
TN = (((0,), (0,)), ((), ()))


def dot(a, b, dims):
    return lax.dot_general(a, b, dims, preferred_element_type=f32)


def doubled(tile, half):
    low = lax.broadcasted_iota(jnp.int32, tile.shape, 1) < HEAD_DIM
    other = pltpu.roll(tile.astype(f32), HEAD_DIM, 1).astype(tile.dtype)
    return jnp.where(low, tile, other) if half == 0 else jnp.where(low, other, tile)


def stack_heads(tiles, kv_half):
    low = lax.broadcasted_iota(jnp.int32, (TQ, 128), 1) < HEAD_DIM
    parts = []
    for a in range(3 * kv_half, 3 * kv_half + 3):
        t = tiles[:, (a // 2) * 128 : (a // 2) * 128 + 128]
        zero = jnp.zeros_like(t)
        parts.append(jnp.where(low, t, zero) if a % 2 == 0 else jnp.where(low, zero, t))
    return jnp.concatenate(parts, axis=0)


def forward_kernel(first_ref, q_ref, k_ref, v_ref, start_ref, out_ref, top_ref, kd, vd, *, most):
    g, i = pl.program_id(0), pl.program_id(1)

    @pl.when(i == 0)
    def _():
        for half in range(2):
            kd[half] = doubled(k_ref[...], half)
            vd[half] = doubled(v_ref[...], half)

    first = first_ref[i]
    count = i + 1 - first
    for width in range(1, most + 1):

        @pl.when(count == width)
        def _(width=width):
            span = width * TQ
            base = pl.multiple_of(first * TQ, TQ)
            row = lax.broadcasted_iota(jnp.int32, (TQ, span), 0) + i * TQ
            col = lax.broadcasted_iota(jnp.int32, (TQ, span), 1) + base
            bias = jnp.where((col <= row) & (col >= start_ref[...]), 0.0, -1e30)
            low = lax.broadcasted_iota(jnp.int32, (TQ, 128), 1) < HEAD_DIM
            tiles = q_ref[...]
            heads = []
            for half in range(2):
                keys = kd[half, pl.ds(base, span), :]
                vals = vd[half, pl.ds(base, span), :]
                s = dot(stack_heads(tiles, half), keys, NT)
                weights, scales = [], []
                for n in range(3):
                    sn = s[n * TQ : n * TQ + TQ] * 0.125 + bias
                    peak = jnp.max(sn, axis=1, keepdims=True)
                    e = jnp.exp(sn - peak)
                    total = jnp.sum(e, axis=1, keepdims=True)
                    a = 3 * half + n
                    top_ref[a] = jnp.broadcast_to(jnp.max(peak, axis=0, keepdims=True), (8, 128))
                    weights.append(e.astype(bf16))
                    scales.append(1.0 / total)
                o = dot(jnp.concatenate(weights, axis=0), vals, NN)
                for n in range(3):
                    heads.append(o[n * TQ : n * TQ + TQ] * scales[n])
            for t in range(3):
                out_ref[:, t * 128 : t * 128 + 128] = jnp.where(low, heads[2 * t], heads[2 * t + 1]).astype(bf16)


def attention_forward(q, k, v, start_col, first, most):
    length = q.shape[0]
    pairs = k.shape[1] // 128
    blocks = length // TQ
    mixed, tops = pl.pallas_call(
        functools.partial(forward_kernel, most=most),
        grid_spec=pltpu.PrefetchScalarGridSpec(
            num_scalar_prefetch=1,
            grid=(pairs, blocks),
            in_specs=[
                pl.BlockSpec((TQ, 384), lambda g, i, s: (i, g)),
                pl.BlockSpec((length, 128), lambda g, i, s: (0, g)),
                pl.BlockSpec((length, 128), lambda g, i, s: (0, g)),
                pl.BlockSpec((TQ, 1), lambda g, i, s: (i, 0)),
            ],
            out_specs=[
                pl.BlockSpec((TQ, 384), lambda g, i, s: (i, g)),
                pl.BlockSpec((None, None, 6, 8, 128), lambda g, i, s: (i, g, 0, 0, 0)),
            ],
            scratch_shapes=[pltpu.VMEM((2, length, 128), bf16), pltpu.VMEM((2, length, 128), bf16)],
        ),
        out_shape=[
            jax.ShapeDtypeStruct(q.shape, bf16),
            jax.ShapeDtypeStruct((blocks, pairs, 6, 8, 128), f32),
        ],
        name="attention_forward",
    )(first, q, k, v, start_col)
    return mixed, jnp.max(tops[:, :, :, 0, 0], axis=0).reshape(pairs * 6)


def unrotate(u, cosine, sine):
    lane = lax.broadcasted_iota(jnp.int32, u.shape, 1)
    swapped = jnp.where(lane % 64 < 32, pltpu.roll(u, 96, 1), pltpu.roll(u, 32, 1))
    return u * cosine - swapped * sine


def backward_kernel(first_ref, q_ref, k_ref, v_ref, g_ref, start_ref, cos_ref, sin_ref, cosall_ref, sinall_ref,
                    dq_ref, dk_ref, dv_ref, kd, vd, dka, dva, *, most):
    g, i = pl.program_id(0), pl.program_id(1)

    @pl.when(i == 0)
    def _():
        for half in range(2):
            kd[half] = doubled(k_ref[...], half)
            vd[half] = doubled(v_ref[...], half)
        dka[...] = jnp.zeros_like(dka)
        dva[...] = jnp.zeros_like(dva)

    first = first_ref[i]
    count = i + 1 - first
    for width in range(1, most + 1):

        @pl.when(count == width)
        def _(width=width):
            span = width * TQ
            base = pl.multiple_of(first * TQ, TQ)
            rows = pl.ds(base, span)
            col = lax.broadcasted_iota(jnp.int32, (span, TQ), 1) + i * TQ
            row = lax.broadcasted_iota(jnp.int32, (span, TQ), 0) + base
            bias = jnp.where((row <= col) & (row >= start_ref[...]), 0.0, -1e30)
            low = lax.broadcasted_iota(jnp.int32, (TQ, 128), 1) < HEAD_DIM
            q_tiles, g_tiles = q_ref[...], g_ref[...]
            heads = []
            for half in range(2):
                keys, vals = kd[half, rows, :], vd[half, rows, :]
                qs, gs = stack_heads(q_tiles, half), stack_heads(g_tiles, half)
                s = dot(keys, qs, NT)
                dp = dot(vals, gs, NT)
                probs, grads = [], []
                for n in range(3):
                    sn = s[:, n * TQ : n * TQ + TQ] * 0.125 + bias
                    peak = jnp.max(sn, axis=0, keepdims=True)
                    e = jnp.exp(sn - peak)
                    soft = e * (1.0 / jnp.sum(e, axis=0, keepdims=True))
                    dpn = dp[:, n * TQ : n * TQ + TQ]
                    inner = jnp.sum(soft * dpn, axis=0, keepdims=True)
                    probs.append(soft.astype(bf16))
                    grads.append((soft * (dpn - inner) * 0.125).astype(bf16))
                p = jnp.concatenate(probs, axis=1)
                ds = jnp.concatenate(grads, axis=1)
                dva[half, rows, :] += dot(p, gs, NN)
                dka[half, rows, :] += dot(ds, qs, NN)
                dq = dot(ds, keys, TN)
                for n in range(3):
                    heads.append(dq[n * TQ : n * TQ + TQ])
            for t in range(3):
                tile = jnp.where(low, heads[2 * t], heads[2 * t + 1])
                dq_ref[:, t * 128 : t * 128 + 128] = unrotate(tile, cos_ref[...], sin_ref[...]).astype(bf16)

    @pl.when(i == pl.num_programs(1) - 1)
    def _():
        def joined(acc):
            a, b = acc[0], acc[1]
            low = lax.broadcasted_iota(jnp.int32, a.shape, 1) < HEAD_DIM
            return jnp.where(low, a + pltpu.roll(a, HEAD_DIM, 1), b + pltpu.roll(b, HEAD_DIM, 1))

        dk_ref[...] = unrotate(joined(dka), cosall_ref[...], sinall_ref[...]).astype(bf16)
        dv_ref[...] = joined(dva).astype(bf16)


def attention_backward(q, k, v, g, start_row, cosine, sine, first, most):
    length = q.shape[0]
    pairs = k.shape[1] // 128
    blocks = length // TQ
    whole = lambda g, i, s: (0, g)
    mine = lambda g, i, s: (i, g)
    return pl.pallas_call(
        functools.partial(backward_kernel, most=most),
        grid_spec=pltpu.PrefetchScalarGridSpec(
            num_scalar_prefetch=1,
            grid=(pairs, blocks),
            in_specs=[
                pl.BlockSpec((TQ, 384), mine),
                pl.BlockSpec((length, 128), whole),
                pl.BlockSpec((length, 128), whole),
                pl.BlockSpec((TQ, 384), mine),
                pl.BlockSpec((1, TQ), lambda g, i, s: (0, i)),
                pl.BlockSpec((TQ, 128), lambda g, i, s: (i, 0)),
                pl.BlockSpec((TQ, 128), lambda g, i, s: (i, 0)),
                pl.BlockSpec((length, 128), lambda g, i, s: (0, 0)),
                pl.BlockSpec((length, 128), lambda g, i, s: (0, 0)),
            ],
            out_specs=[
                pl.BlockSpec((TQ, 384), mine),
                pl.BlockSpec((length, 128), whole),
                pl.BlockSpec((length, 128), whole),
            ],
            scratch_shapes=[pltpu.VMEM((2, length, 128), bf16), pltpu.VMEM((2, length, 128), bf16),
                            pltpu.VMEM((2, length, 128), f32), pltpu.VMEM((2, length, 128), f32)],
        ),
        out_shape=[
            jax.ShapeDtypeStruct(q.shape, bf16),
            jax.ShapeDtypeStruct(k.shape, bf16),
            jax.ShapeDtypeStruct(v.shape, bf16),
        ],
        name="attention_backward",
    )(first, q, k, v, g, start_row, cosine, sine, cosine, sine)


def project_kernel(x_ref, gain_ref, wq_ref, wk_ref, wv_ref, cos_ref, sin_ref, n_ref, q_ref, k_ref, v_ref):
    x = x_ref[...].astype(f32)
    rstd = lax.rsqrt(jnp.mean(x * x, axis=-1, keepdims=True) + eps_norm)
    normed = (x * rstd * gain_ref[...].astype(f32)).astype(bf16)
    n_ref[...] = normed
    cosine, sine = cos_ref[...], -sin_ref[...]
    for w_ref, out_ref in ((wq_ref, q_ref), (wk_ref, k_ref)):
        u = dot(normed, w_ref[...], NN)
        for t in range(out_ref.shape[1] // 128):
            lanes = slice(t * 128, t * 128 + 128)
            out_ref[:, lanes] = unrotate(u[:, lanes], cosine, sine).astype(bf16)
    v_ref[...] = dot(normed, wv_ref[...], NN).astype(bf16)


def project(x, gain, wq, wk, wv, cosine, sine):
    length, width = x.shape
    rows = 256
    row_block = lambda n: pl.BlockSpec((rows, n), lambda i: (i, 0))
    fixed = lambda a: pl.BlockSpec(a.shape, lambda i: (0, 0), pipeline_mode=pl.Buffered(1))
    return pl.pallas_call(
        project_kernel,
        grid=(length // rows,),
        in_specs=[row_block(width), fixed(gain), fixed(wq), fixed(wk), fixed(wv), row_block(128), row_block(128)],
        out_specs=[row_block(width), row_block(wq.shape[1]), row_block(wk.shape[1]), row_block(wv.shape[1])],
        out_shape=[jax.ShapeDtypeStruct((length, n), bf16) for n in (width, wq.shape[1], wk.shape[1], wv.shape[1])],
        name="project",
    )(x, gain, wq, wk, wv, cosine, sine)

def positions_of(segment_row):
    position_index = jnp.arange(segment_row.shape[0], dtype=jnp.int32)
    changed = jnp.concatenate(
        [jnp.ones((1,), dtype=jnp.bool_), segment_row[1:] != segment_row[:-1]]
    )
    starts = lax.cummax(jnp.where(changed, position_index, 0), axis=0)
    return position_index - starts


def rope_tables(places):
    half_size = HEAD_DIM // 2
    frequency = rope_base ** (-jnp.arange(half_size, dtype=jnp.float32) * 2.0 / HEAD_DIM)
    angles = places.astype(jnp.float32)[:, None] * frequency[None, :]
    cosine, sine = jnp.cos(angles), jnp.sin(angles)
    return jnp.concatenate([cosine] * 4, axis=1), jnp.concatenate([-sine, sine, -sine, sine], axis=1)


def product(left, right):
    return jnp.dot(left, right, preferred_element_type=jnp.float32)


def product_left(left, right):
    return lax.dot_general(
        left, right, (((0,), (0,)), ((), ())), preferred_element_type=jnp.float32
    )


def product_right(left, right):
    return lax.dot_general(
        left, right, (((1,), (1,)), ((), ())), preferred_element_type=jnp.float32
    )


def on_device(
    layer_input,
    segments,
    query_weight,
    key_weight,
    value_weight,
    output_weight,
    gate_weight,
    up_weight,
    down_weight,
    attention_gain,
    feedforward_gain,
    upstream,
):
    seq_count, length, model_width = layer_input.shape
    token_rows = seq_count * length
    group_size = HEADS // KV_HEADS
    query_width = HEADS * HEAD_DIM
    key_width = KV_HEADS * HEAD_DIM
    position_index = jnp.arange(length, dtype=jnp.int32)
    query_full, key_full, value_full, output_full, gain_first = (
        lax.all_gather(query_weight, "shard", axis=0, tiled=True),
        lax.all_gather(key_weight, "shard", axis=0, tiled=True),
        lax.all_gather(value_weight, "shard", axis=0, tiled=True),
        lax.all_gather(output_weight, "shard", axis=0, tiled=True),
        lax.all_gather(attention_gain, "shard", axis=0, tiled=True),
    )
    inputs = layer_input.reshape(token_rows, model_width).astype(jnp.float32)
    places = positions_of(segments[0])
    cosine, sine = rope_tables(places)
    doc_start = position_index - places
    first_block = doc_start[::TQ] // TQ
    most = min(length // TQ, MOST_DOC // TQ + 1)
    first_rstd = lax.rsqrt(jnp.mean(inputs * inputs, axis=-1, keepdims=True) + eps_norm)
    first_unit = inputs * first_rstd
    gain_first_wide = gain_first.astype(jnp.float32)
    first_normed, queries, keys_rot, values = project(
        layer_input[0], gain_first[None, :], query_full, key_full, value_full, cosine, sine
    )
    mixed, head_top = attention_forward(
        queries, keys_rot, values, doc_start[:, None], first_block, most
    )
    maxima = lax.pmax(head_top, ("rep", "shard"))
    residual = inputs + product(mixed, output_full)
    gate_full, up_full, down_full, gain_second = (
        lax.all_gather(gate_weight, "shard", axis=0, tiled=True),
        lax.all_gather(up_weight, "shard", axis=0, tiled=True),
        lax.all_gather(down_weight, "shard", axis=0, tiled=True),
        lax.all_gather(feedforward_gain, "shard", axis=0, tiled=True),
    )
    second_rstd = lax.rsqrt(jnp.mean(residual * residual, axis=-1, keepdims=True) + eps_norm)
    second_unit = residual * second_rstd
    gain_second_wide = gain_second.astype(jnp.float32)
    second_normed = (second_unit * gain_second_wide).astype(jnp.bfloat16)
    gate_values = product(second_normed, gate_full)
    up_values = product(second_normed, up_full)
    sigmoid_gate = jax.nn.sigmoid(gate_values)
    swish_gate = gate_values * sigmoid_gate
    activated = (swish_gate * up_values).astype(jnp.bfloat16)
    layer_output = (
        (residual + product(activated, down_full)).astype(jnp.bfloat16).reshape(layer_input.shape)
    )
    gate_back, up_back, down_back = (
        lax.all_gather(gate_weight, "shard", axis=0, tiled=True),
        lax.all_gather(up_weight, "shard", axis=0, tiled=True),
        lax.all_gather(down_weight, "shard", axis=0, tiled=True),
    )
    grad_output = upstream.reshape(token_rows, model_width).astype(jnp.float32)
    grad_down_in = grad_output.astype(jnp.bfloat16)
    grad_activated = product_right(grad_down_in, down_back)
    grad_gate_low = (
        grad_activated * up_values * sigmoid_gate * (1.0 + gate_values * (1.0 - sigmoid_gate))
    ).astype(jnp.bfloat16)
    grad_up_low = (grad_activated * swish_gate).astype(jnp.bfloat16)
    down_term = product_left(activated, grad_down_in)
    gate_term = product_left(second_normed, grad_gate_low)
    up_term = product_left(second_normed, grad_up_low)
    grad_second = product_right(grad_gate_low, gate_back) + product_right(grad_up_low, up_back)
    second_gain_term = jnp.sum(grad_second * second_unit, axis=0)
    grad_unit_second = grad_second * gain_second_wide
    grad_residual = (
        second_rstd
        * (
            grad_unit_second
            - second_unit * jnp.mean(grad_unit_second * second_unit, axis=-1, keepdims=True)
        )
        + grad_output
    )
    feedforward_sums = (
        lax.psum_scatter(
            gate_term.astype(jnp.bfloat16), "shard", scatter_dimension=0, tiled=True
        ),
        lax.psum_scatter(
            up_term.astype(jnp.bfloat16), "shard", scatter_dimension=0, tiled=True
        ),
        lax.psum_scatter(
            down_term.astype(jnp.bfloat16), "shard", scatter_dimension=0, tiled=True
        ),
        lax.psum_scatter(
            second_gain_term.astype(jnp.bfloat16), "shard", scatter_dimension=0, tiled=True
        ),
    )
    gate_grad, up_grad, down_grad, feedforward_gain_grad = (
        lax.psum(part, "rep").astype(jnp.float32) for part in feedforward_sums
    )
    query_back, key_back, value_back, output_back = (
        lax.all_gather(query_weight, "shard", axis=0, tiled=True),
        lax.all_gather(key_weight, "shard", axis=0, tiled=True),
        lax.all_gather(value_weight, "shard", axis=0, tiled=True),
        lax.all_gather(output_weight, "shard", axis=0, tiled=True),
    )
    grad_out_in = grad_residual.astype(jnp.bfloat16)
    output_term = product_left(mixed, grad_out_in)
    grad_mixed = product_right(grad_out_in, output_back).astype(jnp.bfloat16)
    query_low, key_low, value_low = attention_backward(
        queries, keys_rot, values, grad_mixed, doc_start[None, :], cosine, sine, first_block, most
    )
    query_term = product_left(first_normed, query_low)
    key_term = product_left(first_normed, key_low)
    value_term = product_left(first_normed, value_low)
    grad_first = (
        product_right(query_low, query_back)
        + product_right(key_low, key_back)
        + product_right(value_low, value_back)
    )
    first_gain_term = jnp.sum(grad_first * first_unit, axis=0)
    grad_unit_first = grad_first * gain_first_wide
    input_grad = (
        first_rstd
        * (
            grad_unit_first
            - first_unit * jnp.mean(grad_unit_first * first_unit, axis=-1, keepdims=True)
        )
        + grad_residual
    )
    attention_sums = (
        lax.psum_scatter(
            query_term.astype(jnp.bfloat16), "shard", scatter_dimension=0, tiled=True
        ),
        lax.psum_scatter(
            key_term.astype(jnp.bfloat16), "shard", scatter_dimension=0, tiled=True
        ),
        lax.psum_scatter(
            value_term.astype(jnp.bfloat16), "shard", scatter_dimension=0, tiled=True
        ),
        lax.psum_scatter(
            output_term.astype(jnp.bfloat16), "shard", scatter_dimension=0, tiled=True
        ),
        lax.psum_scatter(
            first_gain_term.astype(jnp.bfloat16), "shard", scatter_dimension=0, tiled=True
        ),
    )
    query_grad, key_grad, value_grad, output_grad, attention_gain_grad = (
        lax.psum(part, "rep").astype(jnp.float32) for part in attention_sums
    )
    query_factor = jnp.sqrt(clip_tau / jnp.maximum(maxima, clip_tau))
    key_factor = jnp.sqrt(
        clip_tau / jnp.maximum(jnp.max(maxima.reshape(KV_HEADS, group_size), axis=1), clip_tau)
    )
    local_rows = query_weight.shape[0]
    query_clipped = (
        query_weight.astype(jnp.float32).reshape(local_rows, HEADS, HEAD_DIM)
        * query_factor[None, :, None]
    ).reshape(local_rows, query_width)
    key_clipped = (
        key_weight.astype(jnp.float32).reshape(local_rows, KV_HEADS, HEAD_DIM)
        * key_factor[None, :, None]
    ).reshape(local_rows, key_width)
    return (
        layer_output,
        input_grad.reshape(layer_input.shape),
        query_grad,
        key_grad,
        value_grad,
        output_grad,
        gate_grad,
        up_grad,
        down_grad,
        attention_gain_grad,
        feedforward_gain_grad,
        maxima,
        query_clipped,
        key_clipped,
    )


def solution(mesh):
    return jax.shard_map(
        on_device,
        mesh=mesh,
        in_specs=(
            P(("rep", "shard"), None, None),
            P(("rep", "shard"), None),
            P("shard", None),
            P("shard", None),
            P("shard", None),
            P("shard", None),
            P("shard", None),
            P("shard", None),
            P("shard", None),
            P("shard"),
            P("shard"),
            P(("rep", "shard"), None, None),
        ),
        out_specs=(
            P(("rep", "shard"), None, None),
            P(("rep", "shard"), None, None),
            P("shard", None),
            P("shard", None),
            P("shard", None),
            P("shard", None),
            P("shard", None),
            P("shard", None),
            P("shard", None),
            P("shard"),
            P("shard"),
            P(),
            P("shard", None),
            P("shard", None),
        ),
        check_vma=False,
    )
```

```python
import functools
import math

import jax
import jax.numpy as jnp
from jax import lax
from jax.experimental import pallas as pl
from jax.experimental.pallas import tpu as pltpu
from jax.sharding import PartitionSpec as P

HEADS = 18
KV_HEADS = 6
MOST_DOC = 512
eps_norm = 1e-05
rope_base = 10000.0
clip_tau = 2.5
HEAD_DIM = 64
TQ = 128
f32 = jnp.float32
bf16 = jnp.bfloat16
NT = (((1,), (1,)), ((), ()))
NN = (((1,), (0,)), ((), ()))
TN = (((0,), (0,)), ((), ()))


def dot(a, b, dims):
    return lax.dot_general(a, b, dims, preferred_element_type=f32)


def doubled(tile, half):
    low = lax.broadcasted_iota(jnp.int32, tile.shape, 1) < HEAD_DIM
    other = pltpu.roll(tile.astype(f32), HEAD_DIM, 1).astype(tile.dtype)
    return jnp.where(low, tile, other) if half == 0 else jnp.where(low, other, tile)


def stack_heads(tiles, kv_half):
    low = lax.broadcasted_iota(jnp.int32, (TQ, 128), 1) < HEAD_DIM
    parts = []
    for a in range(3 * kv_half, 3 * kv_half + 3):
        t = tiles[:, (a // 2) * 128 : (a // 2) * 128 + 128]
        zero = jnp.zeros_like(t)
        parts.append(jnp.where(low, t, zero) if a % 2 == 0 else jnp.where(low, zero, t))
    return jnp.concatenate(parts, axis=0)


def forward_kernel(first_ref, q_ref, k_ref, v_ref, start_ref, out_ref, top_ref, kd, vd, *, most):
    g, i = pl.program_id(0), pl.program_id(1)

    @pl.when(i == 0)
    def _():
        for half in range(2):
            kd[half] = doubled(k_ref[...], half)
            vd[half] = doubled(v_ref[...], half)

    first = first_ref[i]
    count = i + 1 - first
    for width in range(1, most + 1):

        @pl.when(count == width)
        def _(width=width):
            span = width * TQ
            base = pl.multiple_of(first * TQ, TQ)
            row = lax.broadcasted_iota(jnp.int32, (TQ, span), 0) + i * TQ
            col = lax.broadcasted_iota(jnp.int32, (TQ, span), 1) + base
            bias = jnp.where((col <= row) & (col >= start_ref[...]), 0.0, -1e30)
            low = lax.broadcasted_iota(jnp.int32, (TQ, 128), 1) < HEAD_DIM
            tiles = q_ref[...]
            heads = []
            for half in range(2):
                keys = kd[half, pl.ds(base, span), :]
                vals = vd[half, pl.ds(base, span), :]
                s = dot(stack_heads(tiles, half), keys, NT)
                weights, scales = [], []
                for n in range(3):
                    sn = s[n * TQ : n * TQ + TQ] * 0.125 + bias
                    peak = jnp.max(sn, axis=1, keepdims=True)
                    e = jnp.exp(sn - peak)
                    total = jnp.sum(e, axis=1, keepdims=True)
                    a = 3 * half + n
                    top_ref[a] = jnp.broadcast_to(jnp.max(peak, axis=0, keepdims=True), (8, 128))
                    weights.append(e.astype(bf16))
                    scales.append(1.0 / total)
                o = dot(jnp.concatenate(weights, axis=0), vals, NN)
                for n in range(3):
                    heads.append(o[n * TQ : n * TQ + TQ] * scales[n])
            for t in range(3):
                out_ref[:, t * 128 : t * 128 + 128] = jnp.where(low, heads[2 * t], heads[2 * t + 1]).astype(bf16)


def attention_forward(q, k, v, start_col, first, most):
    length = q.shape[0]
    pairs = k.shape[1] // 128
    blocks = length // TQ
    mixed, tops = pl.pallas_call(
        functools.partial(forward_kernel, most=most),
        grid_spec=pltpu.PrefetchScalarGridSpec(
            num_scalar_prefetch=1,
            grid=(pairs, blocks),
            in_specs=[
                pl.BlockSpec((TQ, 384), lambda g, i, s: (i, g)),
                pl.BlockSpec((length, 128), lambda g, i, s: (0, g)),
                pl.BlockSpec((length, 128), lambda g, i, s: (0, g)),
                pl.BlockSpec((TQ, 1), lambda g, i, s: (i, 0)),
            ],
            out_specs=[
                pl.BlockSpec((TQ, 384), lambda g, i, s: (i, g)),
                pl.BlockSpec((None, None, 6, 8, 128), lambda g, i, s: (i, g, 0, 0, 0)),
            ],
            scratch_shapes=[pltpu.VMEM((2, length, 128), bf16), pltpu.VMEM((2, length, 128), bf16)],
        ),
        out_shape=[
            jax.ShapeDtypeStruct(q.shape, bf16),
            jax.ShapeDtypeStruct((blocks, pairs, 6, 8, 128), f32),
        ],
        name="attention_forward",
    )(first, q, k, v, start_col)
    return mixed, jnp.max(tops[:, :, :, 0, 0], axis=0).reshape(pairs * 6)


def unrotate(u, cosine, sine):
    lane = lax.broadcasted_iota(jnp.int32, u.shape, 1)
    swapped = jnp.where(lane % 64 < 32, pltpu.roll(u, 96, 1), pltpu.roll(u, 32, 1))
    return u * cosine - swapped * sine


def backward_kernel(first_ref, q_ref, k_ref, v_ref, g_ref, start_ref, cos_ref, sin_ref, cosall_ref, sinall_ref,
                    dq_ref, dk_ref, dv_ref, kd, vd, dka, dva, *, most):
    g, i = pl.program_id(0), pl.program_id(1)

    @pl.when(i == 0)
    def _():
        for half in range(2):
            kd[half] = doubled(k_ref[...], half)
            vd[half] = doubled(v_ref[...], half)
        dka[...] = jnp.zeros_like(dka)
        dva[...] = jnp.zeros_like(dva)

    first = first_ref[i]
    count = i + 1 - first
    for width in range(1, most + 1):

        @pl.when(count == width)
        def _(width=width):
            span = width * TQ
            base = pl.multiple_of(first * TQ, TQ)
            rows = pl.ds(base, span)
            col = lax.broadcasted_iota(jnp.int32, (span, TQ), 1) + i * TQ
            row = lax.broadcasted_iota(jnp.int32, (span, TQ), 0) + base
            bias = jnp.where((row <= col) & (row >= start_ref[...]), 0.0, -1e30)
            low = lax.broadcasted_iota(jnp.int32, (TQ, 128), 1) < HEAD_DIM
            q_tiles, g_tiles = q_ref[...], g_ref[...]
            heads = []
            for half in range(2):
                keys, vals = kd[half, rows, :], vd[half, rows, :]
                qs, gs = stack_heads(q_tiles, half), stack_heads(g_tiles, half)
                s = dot(keys, qs, NT)
                dp = dot(vals, gs, NT)
                probs, grads = [], []
                for n in range(3):
                    sn = s[:, n * TQ : n * TQ + TQ] * 0.125 + bias
                    peak = jnp.max(sn, axis=0, keepdims=True)
                    e = jnp.exp(sn - peak)
                    soft = e * (1.0 / jnp.sum(e, axis=0, keepdims=True))
                    dpn = dp[:, n * TQ : n * TQ + TQ]
                    inner = jnp.sum(soft * dpn, axis=0, keepdims=True)
                    probs.append(soft.astype(bf16))
                    grads.append((soft * (dpn - inner) * 0.125).astype(bf16))
                p = jnp.concatenate(probs, axis=1)
                ds = jnp.concatenate(grads, axis=1)
                dva[half, rows, :] += dot(p, gs, NN)
                dka[half, rows, :] += dot(ds, qs, NN)
                dq = dot(ds, keys, TN)
                for n in range(3):
                    heads.append(dq[n * TQ : n * TQ + TQ])
            for t in range(3):
                tile = jnp.where(low, heads[2 * t], heads[2 * t + 1])
                dq_ref[:, t * 128 : t * 128 + 128] = unrotate(tile, cos_ref[...], sin_ref[...]).astype(bf16)

    @pl.when(i == pl.num_programs(1) - 1)
    def _():
        def joined(acc):
            a, b = acc[0], acc[1]
            low = lax.broadcasted_iota(jnp.int32, a.shape, 1) < HEAD_DIM
            return jnp.where(low, a + pltpu.roll(a, HEAD_DIM, 1), b + pltpu.roll(b, HEAD_DIM, 1))

        dk_ref[...] = unrotate(joined(dka), cosall_ref[...], sinall_ref[...]).astype(bf16)
        dv_ref[...] = joined(dva).astype(bf16)


def attention_backward(q, k, v, g, start_row, cosine, sine, first, most):
    length = q.shape[0]
    pairs = k.shape[1] // 128
    blocks = length // TQ
    whole = lambda g, i, s: (0, g)
    mine = lambda g, i, s: (i, g)
    return pl.pallas_call(
        functools.partial(backward_kernel, most=most),
        grid_spec=pltpu.PrefetchScalarGridSpec(
            num_scalar_prefetch=1,
            grid=(pairs, blocks),
            in_specs=[
                pl.BlockSpec((TQ, 384), mine),
                pl.BlockSpec((length, 128), whole),
                pl.BlockSpec((length, 128), whole),
                pl.BlockSpec((TQ, 384), mine),
                pl.BlockSpec((1, TQ), lambda g, i, s: (0, i)),
                pl.BlockSpec((TQ, 128), lambda g, i, s: (i, 0)),
                pl.BlockSpec((TQ, 128), lambda g, i, s: (i, 0)),
                pl.BlockSpec((length, 128), lambda g, i, s: (0, 0)),
                pl.BlockSpec((length, 128), lambda g, i, s: (0, 0)),
            ],
            out_specs=[
                pl.BlockSpec((TQ, 384), mine),
                pl.BlockSpec((length, 128), whole),
                pl.BlockSpec((length, 128), whole),
            ],
            scratch_shapes=[pltpu.VMEM((2, length, 128), bf16), pltpu.VMEM((2, length, 128), bf16),
                            pltpu.VMEM((2, length, 128), f32), pltpu.VMEM((2, length, 128), f32)],
        ),
        out_shape=[
            jax.ShapeDtypeStruct(q.shape, bf16),
            jax.ShapeDtypeStruct(k.shape, bf16),
            jax.ShapeDtypeStruct(v.shape, bf16),
        ],
        name="attention_backward",
    )(first, q, k, v, g, start_row, cosine, sine, cosine, sine)


def cost(flops, arrays):
    return pl.CostEstimate(
        flops=int(flops // 8), transcendentals=0, bytes_accessed=int(sum(a.size * a.dtype.itemsize for a in arrays) // 8)
    )


def shape(rows, columns, kind=bf16):
    return jax.ShapeDtypeStruct((rows, columns), kind)


ANY = pl.BlockSpec(memory_space=pl.ANY)


class Pieces:
    def __init__(self, rows, columns):
        self.rows, self.columns, self.parts = rows, columns, []

    def arrays(self):
        return [a for a, _, _ in self.parts]

    def places(self):
        return [(m, h) for _, m, h in self.parts]


def piece_copies(refs, places, rows, target, sems, me, columns=None):
    copies = []
    for n, (ref, (m, h)) in enumerate(zip(refs, places)):
        at = jnp.bitwise_xor(me[0], m) * rows
        if h is not None:
            at = at + jnp.bitwise_xor(jnp.bitwise_and(me[1], 1), h) * (rows // 2)
        source = ref if columns is None else ref.at[:, columns]
        place = target.at[pl.ds(pl.multiple_of(at, 16), ref.shape[0]), :]
        copies.append(pltpu.make_async_copy(source, place, sems.at[n]))
    return copies


def other_ways(axis, bit):
    size = lax.axis_size(axis)
    return [(n, n ^ bit) for n in range(size)]


def swap(value, axis, bit):
    return lax.ppermute(value, axis, other_ways(axis, bit))


class Spread(Pieces):
    def __init__(self, weight, *tokens):
        rows = weight.shape[0]
        super().__init__(rows, weight.shape[1])
        source = then(weight, *tokens) if tokens else weight
        odd = jnp.bitwise_and(lax.axis_index("rep"), 1)
        half = lax.dynamic_slice_in_dim(source, odd * (rows // 2), rows // 2, 0)
        self.near = swap(half, "shard", 2)
        self.parts = [(weight, 0, None), (swap(source, "shard", 1), 1, None)]

    def forward(self, *tokens):
        near = then(self.near, *tokens) if tokens else self.near
        self.far = swap(near, "rep", 1)
        self.parts += [(near, 2, 0), (swap(near, "shard", 1), 3, 0)]

    def finish(self, *tokens):
        far = then(self.far, *tokens) if tokens else self.far
        self.parts += [(far, 2, 1), (swap(far, "shard", 1), 3, 1)]


def dense_call(body, me, grid, blocked, resident, weights, outs, name, flops, scratch=()):
    counts = [len(w.parts) for w in weights]

    def kernel(me_ref, *refs):
        refs = list(refs)

        def take(n):
            got = refs[:n]
            del refs[:n]
            return got

        b_refs, r_refs = take(len(blocked)), take(len(resident))
        w_refs = [take(n) for n in counts]
        o_refs = take(len(outs))
        targets = take(len(weights))
        sems = take(len(weights))
        copies = [
            piece_copies(r, w.places(), w.rows, t, s, me_ref)
            for r, w, t, s in zip(w_refs, weights, targets, sems)
        ]

        @pl.when(pl.program_id(0) == 0)
        def _():
            for group in copies:
                for c in group:
                    c.start()
            for group in copies:
                for c in group:
                    c.wait()

        body(b_refs, r_refs, targets, o_refs, refs)

    fixed = lambda a: pl.BlockSpec(a.shape, lambda i, s: (0,) * a.ndim, pipeline_mode=pl.Buffered(1))
    arrays = [a for a, _ in blocked] + list(resident) + [a for w in weights for a in w.arrays()]
    return pl.pallas_call(
        kernel,
        grid_spec=pltpu.PrefetchScalarGridSpec(
            num_scalar_prefetch=1,
            grid=(grid,),
            in_specs=[s for _, s in blocked] + [fixed(a) for a in resident] + [ANY] * sum(counts),
            out_specs=[s for _, s in outs],
            scratch_shapes=[pltpu.VMEM((4 * w.rows, w.columns), bf16) for w in weights]
            + [pltpu.SemaphoreType.DMA((n,)) for n in counts]
            + list(scratch),
        ),
        out_shape=[a for a, _ in outs],
        cost_estimate=cost(flops, arrays + [a for a, _ in outs]),
        name=name,
    )(me, *arrays)


ROWS = 256


def rows_of(n):
    return pl.BlockSpec((ROWS, n), lambda i, s: (i, 0))


def project(me, x, gain, wq, wkv, cosine, sine):
    length, width = x.shape
    kv = wkv.columns // 2

    def body(blocked, resident, weights, outs, _):
        x_ref, cos_ref, sin_ref = blocked
        n_ref, q_ref, k_ref, v_ref = outs
        u = x_ref[...].astype(f32)
        rstd = lax.rsqrt(jnp.mean(u * u, axis=-1, keepdims=True) + eps_norm)
        normed = (u * rstd * resident[0][...]).astype(bf16)
        n_ref[...] = normed
        c, s = cos_ref[...], -sin_ref[...]
        q = dot(normed, weights[0][...], NN)
        k = dot(normed, weights[1][...], NN)
        for out_ref, y in ((q_ref, q), (k_ref, k)):
            for t in range(out_ref.shape[1] // 128):
                lanes = slice(t * 128, t * 128 + 128)
                out_ref[:, lanes] = unrotate(y[:, lanes], c, s).astype(bf16)
        v_ref[...] = k[:, kv:].astype(bf16)

    outs = [(shape(length, n), rows_of(n)) for n in (width, wq.columns, kv, kv)]
    blocked = [(x, rows_of(width)), (cosine, rows_of(128)), (sine, rows_of(128))]
    return dense_call(
        body, me, length // ROWS, blocked, [gain], [wq, wkv], outs, "project",
        2 * length * width * (wq.columns + wkv.columns),
    )


def attend_out(me, mixed, x, gain, wo):
    length, width = x.shape

    def body(blocked, resident, weights, outs, _):
        r = blocked[1][...].astype(f32) + dot(blocked[0][...], weights[0][...], NN)
        rstd = lax.rsqrt(jnp.mean(r * r, axis=-1, keepdims=True) + eps_norm)
        outs[0][...] = r
        outs[1][...] = (r * rstd * resident[0][...]).astype(bf16)

    outs = [(shape(length, width, f32), rows_of(width)), (shape(length, width), rows_of(width))]
    blocked = [(mixed, rows_of(mixed.shape[1])), (x, rows_of(width))]
    return dense_call(
        body, me, length // ROWS, blocked, [gain], [wo], outs, "attend_out", 2 * length * width * mixed.shape[1]
    )


def feed_forward(me, normed, grad_y, gate, up, down):
    length, width = normed.shape
    tile = down.rows
    steps = gate.columns // tile
    counts = [len(gate.parts), len(up.parts), len(down.parts)]

    def kernel(me_ref, n_ref, y_ref, *refs):
        refs = list(refs)
        g_parts, u_parts, d_parts = (
            [refs.pop(0) for _ in range(counts[0])],
            [refs.pop(0) for _ in range(counts[1])],
            [refs.pop(0) for _ in range(counts[2])],
        )
        act_ref, gg_ref, gu_ref, wg, wu, wd, g_sem, u_sem, d_sem = refs
        step = pl.program_id(0)

        def transfer(t, what):
            slot = lax.rem(t, 2)
            columns = pl.ds(pl.multiple_of(t * tile, 128), tile)
            for parts, w, sem, target in ((g_parts, gate, g_sem, wg), (u_parts, up, u_sem, wu)):
                for c in piece_copies(parts, w.places(), w.rows, target.at[slot], sem.at[slot], me_ref, columns):
                    getattr(c, what)()
            block = jnp.bitwise_xor(me_ref[0], t)
            odd = jnp.bitwise_and(me_ref[1], 1)
            for n, (ref, (m, h)) in enumerate(zip(d_parts, down.places())):

                @pl.when(block == m)
                def _(n=n, ref=ref, h=h):
                    at = 0 if h is None else pl.multiple_of(jnp.bitwise_xor(odd, h) * (tile // 2), 16)
                    place = wd.at[slot, pl.ds(at, ref.shape[0]), :]
                    getattr(pltpu.make_async_copy(ref, place, d_sem.at[slot, n]), what)()

        @pl.when(step == 0)
        def _():
            transfer(step, "start")

        @pl.when(step + 1 < steps)
        def _():
            transfer(step + 1, "start")

        transfer(step, "wait")
        slot = lax.rem(step, 2)

        @pl.loop(0, length // ROWS)
        def _(r):
            rows = pl.ds(pl.multiple_of(r * ROWS, ROWS), ROWS)
            n = n_ref[rows, :]
            g = dot(n, wg[slot], NN)
            u = dot(n, wu[slot], NN)
            ga = dot(y_ref[rows, :], wd[slot], NT)
            s = 1.0 / (1.0 + jnp.exp(-g))
            swish = g * s
            act_ref[rows, :] = (swish * u).astype(bf16)
            gg_ref[rows, :] = (ga * u * s * (1.0 + g * (1.0 - s))).astype(bf16)
            gu_ref[rows, :] = (ga * swish).astype(bf16)

    whole = pl.BlockSpec((length, width), lambda t, s: (0, 0), pipeline_mode=pl.Buffered(1))
    out = pl.BlockSpec((length, tile), lambda t, s: (0, t))
    arrays = gate.arrays() + up.arrays() + down.arrays()
    outs = [shape(length, gate.columns)] * 3
    return pl.pallas_call(
        kernel,
        grid_spec=pltpu.PrefetchScalarGridSpec(
            num_scalar_prefetch=1,
            grid=(steps,),
            in_specs=[whole, whole] + [ANY] * len(arrays),
            out_specs=[out] * 3,
            scratch_shapes=[
                pltpu.VMEM((2, width, tile), bf16),
                pltpu.VMEM((2, width, tile), bf16),
                pltpu.VMEM((2, tile, width), bf16),
            ]
            + [pltpu.SemaphoreType.DMA((2, n)) for n in counts],
        ),
        out_shape=outs,
        cost_estimate=cost(6 * length * width * gate.columns, [normed, grad_y] + arrays + outs),
        name="feed_forward",
    )(me, normed, grad_y, *arrays)


def norm_backward(grad, unit, rstd, gain):
    scaled = grad * gain
    return rstd * (scaled - unit * jnp.mean(scaled * unit, axis=-1, keepdims=True))


def add_rows(ref, value):
    @pl.when(pl.program_id(0) == 0)
    def _():
        ref[...] = jnp.zeros_like(ref)

    ref[...] += jnp.sum(value, axis=0, keepdims=True)


def feed_forward_back(me, grad_gate, grad_up, residual, grad_y, gain, gate, up, wo):
    length, width = residual.shape

    def body(blocked, resident, weights, outs, _):
        gs = dot(blocked[0][...], weights[0][...], NT) + dot(blocked[1][...], weights[1][...], NT)
        r = blocked[2][...]
        rstd = lax.rsqrt(jnp.mean(r * r, axis=-1, keepdims=True) + eps_norm)
        unit = r * rstd
        add_rows(outs[3], gs * unit)
        gr = norm_backward(gs, unit, rstd, resident[0][...]) + blocked[3][...].astype(f32)
        low = gr.astype(bf16)
        outs[0][...] = gr
        outs[1][...] = low
        outs[2][...] = dot(low, weights[2][...], NT).astype(bf16)

    heads = 4 * wo.rows
    outs = [
        (shape(length, width, f32), rows_of(width)),
        (shape(length, width), rows_of(width)),
        (shape(length, heads), rows_of(heads)),
        (shape(1, width, f32), pl.BlockSpec((1, width), lambda i, s: (0, 0))),
    ]
    ff = gate.columns
    blocked = [(grad_gate, rows_of(ff)), (grad_up, rows_of(ff)), (residual, rows_of(width)), (grad_y, rows_of(width))]
    return dense_call(
        body, me, length // ROWS, blocked, [gain], [gate, up, wo], outs, "feed_forward_back",
        2 * length * width * (2 * ff + heads),
    )


def layer_out(me, activated, residual, down):
    length, width = residual.shape

    def body(blocked, resident, weights, outs, _):
        outs[0][...] = (blocked[1][...] + dot(blocked[0][...], weights[0][...], NN)).astype(bf16)

    ff = activated.shape[1]
    blocked = [(activated, rows_of(ff)), (residual, rows_of(width))]
    return dense_call(
        body, me, length // ROWS, blocked, [], [down], [(shape(length, width), rows_of(width))], "layer_out",
        2 * length * width * ff,
    )[0]


def input_back(me, dq, dk, dv, x, grad_residual, gain, wq, wkv):
    length, width = x.shape

    def body(blocked, resident, weights, outs, _):
        kv = jnp.concatenate([blocked[1][...], blocked[2][...]], axis=1)
        gf = dot(blocked[0][...], weights[0][...], NT) + dot(kv, weights[1][...], NT)
        u = blocked[3][...].astype(f32)
        rstd = lax.rsqrt(jnp.mean(u * u, axis=-1, keepdims=True) + eps_norm)
        unit = u * rstd
        add_rows(outs[1], gf * unit)
        outs[0][...] = norm_backward(gf, unit, rstd, resident[0][...]) + blocked[4][...]

    blocked = [(a, rows_of(a.shape[1])) for a in (dq, dk, dv, x, grad_residual)]
    outs = [
        (shape(length, width, f32), rows_of(width)),
        (shape(1, width, f32), pl.BlockSpec((1, width), lambda i, s: (0, 0))),
    ]
    return dense_call(
        body, me, length // ROWS, blocked, [gain], [wq, wkv], outs, "input_back",
        2 * length * width * (wq.columns + wkv.columns),
    )


def weight_grad(me, left, rights, tile, name):
    length, rows = left.shape
    quarter = rows // 4
    tiles = [r.shape[1] // tile for r in rights]
    firsts = [sum(tiles[:n]) for n in range(len(tiles))]
    steps = sum(tiles)

    def kernel(me_ref, l_ref, *refs):
        r_refs, (near_ref, own_ref, cross_ref), held = refs[: len(rights)], refs[len(rights) : -1], refs[-1]
        step = pl.program_id(0)
        for first, count, r_ref in zip(firsts, tiles, r_refs):

            @pl.when((step >= first) & (step < first + count))
            def _(r_ref=r_ref):
                held[...] = dot(l_ref[...], r_ref[...], TN).astype(bf16)

        def block(m):
            at = pl.multiple_of(jnp.bitwise_xor(me_ref[0], m) * quarter, 16)
            return held[pl.ds(at, quarter), :]

        near_ref[:quarter, :] = block(1)
        near_ref[quarter:, :] = block(3)
        own_ref[...] = block(0)
        cross_ref[...] = block(2)

    def right_spec(first, count):
        return pl.BlockSpec((length, tile), lambda j, s: (0, jnp.clip(j - first, 0, count - 1)))

    heights = (2 * quarter, quarter, quarter)
    outs = [shape(h, steps * tile) for h in heights]
    return pl.pallas_call(
        kernel,
        grid_spec=pltpu.PrefetchScalarGridSpec(
            num_scalar_prefetch=1,
            grid=(steps,),
            in_specs=[pl.BlockSpec((length, rows), lambda j, s: (0, 0), pipeline_mode=pl.Buffered(1))]
            + [right_spec(f, c) for f, c in zip(firsts, tiles)],
            out_specs=[pl.BlockSpec((h, tile), lambda j, s: (0, j)) for h in heights],
            scratch_shapes=[pltpu.VMEM((rows, tile), bf16)],
        ),
        out_shape=outs,
        cost_estimate=cost(2 * length * rows * steps * tile, [left, *rights] + outs),
        name=name,
    )(me, left, *rights)


def wide_sum(*values):
    total = values[0].astype(f32)
    for v in values[1:]:
        total = total + v.astype(f32)
    return total.astype(bf16)


def then(values, *tokens):
    return lax.optimization_barrier((values, tokens))[0]


MESH = pl.DeviceIdType.MESH


def rep_sums(chunks, small):
    units, outs, flat, maps = [], [], [], []
    for terms, unit, order in chunks:
        where = []
        for arrays in terms:
            rows, columns = arrays[0].shape
            for r in range(rows // unit[0]):
                for c in range(columns // unit[1]):
                    where.append((len(flat), len(arrays), r * unit[0], c * unit[1]))
            flat += arrays
        maps.append(where)
        tall = terms[0][0].shape[1] == unit[1]
        outs.append(shape(unit[0] * 8, unit[1]) if tall else shape(unit[0], unit[1] * 8))
        units.append((unit, tall, order))
    count = len(chunks)

    def kernel(*refs):
        ins, small_ref = refs[: len(flat)], refs[len(flat)]
        out_refs = refs[len(flat) + 1 : len(flat) + 1 + count]
        small_out = refs[len(flat) + 1 + count]
        rest = list(refs[len(flat) + 2 + count :])
        held = [rest.pop(0) for _ in range(count)]
        landed = [rest.pop(0) for _ in range(count)]
        load_sem, send_sem, recv_sem, own_sem, small_held, small_landed, small_send, small_recv = rest
        me, shard = lax.axis_index("rep"), lax.axis_index("shard")
        x = lambda d: jnp.bitwise_xor(me, d)

        for c in range(count):
            for u, (first, terms, r, k) in enumerate(maps[c]):
                for t in range(terms):
                    unit = units[c][0]
                    source = ins[first + t].at[pl.ds(r, unit[0]), pl.ds(k, unit[1])]
                    pltpu.make_async_copy(source, held[c].at[t, u], load_sem.at[c, t, u]).start()
        small_held[0] = small_ref[...]

        barrier = pltpu.get_barrier_semaphore()
        peers = [{"rep": x(1)}, {"rep": x(2)}, {"rep": x(4)}]
        peers += [{"shard": jnp.bitwise_xor(shard, 1)}, {"shard": jnp.bitwise_xor(shard, 2)}]
        for peer in peers:
            pl.semaphore_signal(barrier, inc=1, device_id=peer, device_id_type=MESH)
        pl.semaphore_wait(barrier, len(peers))

        def send(source, target, c, n, bit):
            return pltpu.make_async_remote_copy(
                src_ref=source, dst_ref=target, send_sem=send_sem.at[c, n], recv_sem=recv_sem.at[c, n],
                device_id={"rep": x(bit)}, device_id_type=MESH,
            )

        def place(c, u):
            unit, tall, _ = units[c]
            if tall:
                return out_refs[c].at[pl.ds(pl.multiple_of(u * unit[0], 16), unit[0]), :]
            return out_refs[c].at[:, pl.ds(pl.multiple_of(u * unit[1], 128), unit[1])]

        def plan(c):
            bits = units[c][2]
            kept = list(range(8))
            stages = []
            for bit in bits:
                kept = [d for d in kept if not d & bit]
                stages.append((bit, kept))
            return stages

        def reduce_copies(c, j):
            bit, kept = plan(c)[j]
            first = [0, 4, 6][j]
            return [send(held[c].at[0, x(d | bit)], landed[c].at[first + i], c, first + i, bit) for i, d in enumerate(kept)]

        def give_copies(c, j):
            bit, kept = plan(c)[j]
            first = 7 + [0, 4, 6][j]
            return [send(place(c, x(d)), place(c, x(d)), c, first + i, bit) for i, d in enumerate(kept)]

        def small_copy(j):
            return pltpu.make_async_remote_copy(
                src_ref=small_held.at[j], dst_ref=small_landed.at[j], send_sem=small_send.at[j], recv_sem=small_recv.at[j],
                device_id=peers[j], device_id_type=MESH,
            )

        def small_step(j):
            small_copy(j).wait()
            a, b = small_held[j], small_landed[j]
            row = lax.broadcasted_iota(jnp.int32, a.shape, 0)
            small_held[j + 1] = jnp.where(row == 2, jnp.maximum(a, b), a + b)
            if j < 4:
                small_copy(j + 1).start()

        small_copy(0).start()
        for c in range(count):
            for u, (first, terms, r, k) in enumerate(maps[c]):
                for t in range(terms):
                    unit = units[c][0]
                    source = ins[first + t].at[pl.ds(r, unit[0]), pl.ds(k, unit[1])]
                    pltpu.make_async_copy(source, held[c].at[t, u], load_sem.at[c, t, u]).wait()
            terms = maps[c][0][1]

            @pl.loop(0, 8)
            def _(u, c=c, terms=terms):
                held[c][0, u] = wide_sum(*[held[c][t, u] for t in range(terms)])

            for copy in reduce_copies(c, 0):
                copy.start()
        for j in range(3):
            small_step(j)
            for c in range(count):
                bit, kept = plan(c)[j]
                first = [0, 4, 6][j]
                for i, (d, copy) in enumerate(zip(kept, reduce_copies(c, j))):
                    copy.wait()
                    held[c][0, x(d)] = wide_sum(held[c][0, x(d)], landed[c][first + i])
                if j < 2:
                    for copy in reduce_copies(c, j + 1):
                        copy.start()
                else:
                    own = pltpu.make_async_copy(held[c].at[0, me], place(c, me), own_sem.at[c])
                    own.start()
                    own.wait()
                    for copy in give_copies(c, 2):
                        copy.start()
        for j in (2, 1, 0):
            if j:
                small_step(5 - j)
            for c in range(count):
                for copy in give_copies(c, j):
                    copy.wait()
                if j:
                    for copy in give_copies(c, j - 1):
                        copy.start()
        small_out[...] = small_held[5]

    scratch = [pltpu.VMEM((len(terms[0]), 8) + unit, bf16) for terms, unit, _ in chunks]
    scratch += [pltpu.VMEM((7,) + unit, bf16) for _, unit, _ in chunks]
    most = max(len(terms[0]) for terms, _, _ in chunks)
    scratch += [
        pltpu.SemaphoreType.DMA((count, most, 8)),
        pltpu.SemaphoreType.DMA((count, 14)),
        pltpu.SemaphoreType.DMA((count, 14)),
        pltpu.SemaphoreType.DMA((count,)),
        pltpu.VMEM((6,) + small.shape, f32),
        pltpu.VMEM((5,) + small.shape, f32),
        pltpu.SemaphoreType.DMA((5,)),
        pltpu.SemaphoreType.DMA((5,)),
    ]
    vmem = pl.BlockSpec(memory_space=pltpu.VMEM)
    return pl.pallas_call(
        kernel,
        in_specs=[ANY] * len(flat) + [vmem],
        out_specs=[ANY] * count + [vmem],
        out_shape=outs + [shape(*small.shape, f32)],
        scratch_shapes=scratch,
        compiler_params=pltpu.CompilerParams(collective_id=0, has_side_effects=True),
        name="rep_sums",
    )(*flat, small)


def small_all(value, is_max):
    for axis in ("shard", "rep"):
        bit = 1
        while bit < lax.axis_size(axis):
            other = swap(value, axis, bit)
            value = jnp.where(is_max, jnp.maximum(value, other), value + other)
            bit *= 2
    return value


def positions_of(segment_row):
    position_index = jnp.arange(segment_row.shape[0], dtype=jnp.int32)
    changed = jnp.concatenate(
        [jnp.ones((1,), dtype=jnp.bool_), segment_row[1:] != segment_row[:-1]]
    )
    starts = lax.cummax(jnp.where(changed, position_index, 0), axis=0)
    return position_index - starts


def rope_tables(places):
    half_size = HEAD_DIM // 2
    frequency = rope_base ** (-jnp.arange(half_size, dtype=jnp.float32) * 2.0 / HEAD_DIM)
    angles = places.astype(jnp.float32)[:, None] * frequency[None, :]
    cosine, sine = jnp.cos(angles), jnp.sin(angles)
    return jnp.concatenate([cosine] * 4, axis=1), jnp.concatenate([-sine, sine, -sine, sine], axis=1)


def in_order(parts):
    index = lax.axis_index("shard")
    even, odd = jnp.bitwise_and(index, 1) == 0, jnp.bitwise_and(index, 2) == 0
    a, b, c, d = parts
    a, b, c, d = jnp.where(even, a, b), jnp.where(even, b, a), jnp.where(even, c, d), jnp.where(even, d, c)
    return [jnp.where(odd, a, c), jnp.where(odd, b, d), jnp.where(odd, c, a), jnp.where(odd, d, b)]


def on_device(
    layer_input,
    segments,
    query_weight,
    key_weight,
    value_weight,
    output_weight,
    gate_weight,
    up_weight,
    down_weight,
    attention_gain,
    feedforward_gain,
    upstream,
):
    _, length, model_width = layer_input.shape
    query_width, key_width = query_weight.shape[1], key_weight.shape[1]
    shard, rep = lax.axis_index("shard"), lax.axis_index("rep")
    me = jnp.stack([shard, rep]).astype(jnp.int32)
    x, grad_y = layer_input[0], upstream[0]

    gains = jnp.stack([attention_gain, feedforward_gain])
    gains = jnp.concatenate(
        in_order([gains] + [swap(gains, "shard", m) for m in (1, 2, 3)]), axis=1
    ).astype(f32)
    wkv = Spread(jnp.concatenate([key_weight, value_weight], axis=1))
    wq = Spread(query_weight)
    for w in (wkv, wq):
        w.forward()
    for w in (wkv, wq):
        w.finish()
    wo = Spread(output_weight, wq.near)
    gate, up, down = (Spread(w, wq.near) for w in (gate_weight, up_weight, down_weight))

    position_index = jnp.arange(length, dtype=jnp.int32)
    places = positions_of(segments[0])
    cosine, sine = rope_tables(places)
    doc_start = position_index - places
    first_block = doc_start[::TQ] // TQ
    most = min(length // TQ, MOST_DOC // TQ + 1)

    first_normed, queries, keys, values = project(me, x, gains[:1], wq, wkv, cosine, sine)
    for w in (wo, gate):
        w.forward(values)
    mixed, head_top = attention_forward(
        then(queries, wo.near, gate.near), keys, values, doc_start[:, None], first_block, most
    )
    wo.finish(mixed)
    gate.finish(mixed)
    up.forward(mixed)
    down.forward(mixed)
    residual, second_normed = attend_out(me, then(mixed, up.near, down.near), x, gains[1:], wo)
    up.finish(second_normed)
    down.finish(second_normed)
    activated, grad_gate, grad_up = feed_forward(me, second_normed, grad_y, gate, up, down)

    class Sum:
        def __init__(self, blocks):
            self.near, self.own, self.cross = blocks
            self.rows = self.own.shape[0]
            self.got = swap(self.near, "shard", 1)

        def cross_over(self, *tokens):
            got = then(self.got, *tokens)
            self.own_near, sent = got, wide_sum(self.cross, got[self.rows :])
            self.sent = sent
            self.crossed = swap(sent, "shard", 2)

        def terms(self):
            return [self.own, self.own_near, self.crossed]

    gate_sum = Sum(weight_grad(me, second_normed, [grad_gate], 512, "gate_grad"))
    up_sum = Sum(weight_grad(me, then(second_normed, gate_sum.own), [grad_up], 512, "up_grad"))
    gate_sum.cross_over(up_sum.own)
    down_sum = Sum(weight_grad(me, then(activated, gate_sum.sent), [grad_y], 384, "down_grad"))
    up_sum.cross_over(down_sum.own)
    grad_residual, grad_low, grad_mixed, second_gain = feed_forward_back(
        me, then(grad_gate, up_sum.sent), grad_up, residual, grad_y, gains[1:], gate, up, wo
    )
    down_sum.cross_over(grad_low)
    output_sum = Sum(weight_grad(me, then(mixed, down_sum.sent), [grad_low], 384, "output_grad"))
    dq, dk, dv = attention_backward(
        then(queries, output_sum.own, gate_sum.crossed), keys, values, grad_mixed, doc_start[None, :], cosine, sine, first_block, most
    )
    output_sum.cross_over(dq)
    qkv_sum = Sum(weight_grad(me, then(first_normed, output_sum.sent, up_sum.crossed), [dq, dk, dv], 384, "qkv_grad"))
    input_grad, first_gain = input_back(
        me, then(dq, qkv_sum.own), dk, dv, x, grad_residual, gains[:1], wq, wkv
    )
    qkv_sum.cross_over(first_gain)
    layer_output = layer_out(me, then(activated, qkv_sum.sent, down_sum.crossed, output_sum.crossed), residual, down)

    top = jnp.full((1, model_width), -1e30, f32).at[0, :HEADS].set(head_top)
    small = jnp.concatenate([first_gain, second_gain, top, jnp.zeros((5, model_width), f32)], axis=0)
    if lax.axis_size("rep") == 8:
        wide, narrow = (gate_sum.rows, gate_weight.shape[1] // 8), (down_sum.rows // 8, model_width)
        chunks = [
            ([gate_sum.terms()], wide, (1, 2, 4)),
            ([up_sum.terms()], wide, (2, 4, 1)),
            ([down_sum.terms()], narrow, (1, 2, 4)),
            ([output_sum.terms(), qkv_sum.terms()], wide, (2, 4, 1)),
        ]
        gate_grad, up_grad, down_grad, attention, small = rep_sums(chunks, then(small, layer_output))
        output_grad, qkv_grad = attention[:, :model_width], attention[:, model_width:]
    else:
        gate_grad, up_grad, down_grad, output_grad, qkv_grad = (
            lax.psum(wide_sum(v.own, v.own_near[: v.rows], v.crossed), "rep") for v in (gate_sum, up_sum, down_sum, output_sum, qkv_sum)
        )
        small = small_all(small, jnp.arange(8)[:, None] == 2)
    gate_grad, up_grad, down_grad, output_grad, qkv_grad = (
        v.astype(f32) for v in (gate_grad, up_grad, down_grad, output_grad, qkv_grad)
    )
    maxima = small[2, :HEADS]
    own = attention_gain.shape[0]
    attention_gain_grad = lax.dynamic_slice(small[0], (shard * own,), (own,))
    feedforward_gain_grad = lax.dynamic_slice(small[1], (shard * own,), (own,))
    query_grad = qkv_grad[:, :query_width]
    key_grad = qkv_grad[:, query_width : query_width + key_width]
    value_grad = qkv_grad[:, query_width + key_width : query_width + 2 * key_width]
    group_size = HEADS // KV_HEADS
    query_factor = jnp.sqrt(clip_tau / jnp.maximum(maxima, clip_tau))
    key_factor = jnp.sqrt(
        clip_tau / jnp.maximum(jnp.max(maxima.reshape(KV_HEADS, group_size), axis=1), clip_tau)
    )
    local_rows = query_weight.shape[0]
    query_clipped = (
        query_weight.astype(jnp.float32).reshape(local_rows, HEADS, HEAD_DIM)
        * query_factor[None, :, None]
    ).reshape(local_rows, query_width)
    key_clipped = (
        key_weight.astype(jnp.float32).reshape(local_rows, KV_HEADS, HEAD_DIM)
        * key_factor[None, :, None]
    ).reshape(local_rows, key_width)
    return (
        layer_output.reshape(layer_input.shape),
        input_grad.reshape(layer_input.shape),
        query_grad,
        key_grad,
        value_grad,
        output_grad,
        gate_grad,
        up_grad,
        down_grad,
        attention_gain_grad,
        feedforward_gain_grad,
        maxima,
        query_clipped,
        key_clipped,
    )


def solution(mesh):
    return jax.shard_map(
        on_device,
        mesh=mesh,
        in_specs=(
            P(("rep", "shard"), None, None),
            P(("rep", "shard"), None),
            P("shard", None),
            P("shard", None),
            P("shard", None),
            P("shard", None),
            P("shard", None),
            P("shard", None),
            P("shard", None),
            P("shard"),
            P("shard"),
            P(("rep", "shard"), None, None),
        ),
        out_specs=(
            P(("rep", "shard"), None, None),
            P(("rep", "shard"), None, None),
            P("shard", None),
            P("shard", None),
            P("shard", None),
            P("shard", None),
            P("shard", None),
            P("shard", None),
            P("shard", None),
            P("shard"),
            P("shard"),
            P(),
            P("shard", None),
            P("shard", None),
        ),
        check_vma=False,
    )
```
